32 devices in a mesh: dp: 4 (over x, core), fsdp: 8 (over z, y).
Axes of the slice: x: 2, y: 2, z: 4, core: 2. Of those that a mesh axis runs over, the one named last changes fastest.
Arguments:
- tokens: bfloat16 [64, 512, 768], P(('dp', 'fsdp')), may hold values from -6 to 6
- teacher: bfloat16 [64, 512, 768], P(('dp', 'fsdp')), may hold values from -6 to 6
- lengths: int32 [64], P(('dp', 'fsdp')), may hold values from 128 to 512, as said below
- w_query: bfloat16 [768, 768], P(('dp', 'fsdp')), may hold values from -0.109375 to 0.109375
- w_key: bfloat16 [768, 768], P(('dp', 'fsdp')), may hold values from -0.109375 to 0.109375
- w_value: bfloat16 [768, 768], P(('dp', 'fsdp')), may hold values from -0.21875 to 0.21875
- w_out: bfloat16 [768, 768], P(('dp', 'fsdp')), may hold values from -0.4375 to 0.4375
- w_gate: bfloat16 [768, 3072], P(('dp', 'fsdp')), may hold values from -0.21875 to 0.21875
- w_up: bfloat16 [768, 3072], P(('dp', 'fsdp')), may hold values from -0.21875 to 0.21875
- w_down: bfloat16 [3072, 768], P(('dp', 'fsdp')), may hold values from -0.15625 to 0.15625
- gain_attn: bfloat16 [768], P(('dp', 'fsdp')), may hold values from 0.099609375 to 1.8984375
- gain_ff: bfloat16 [768], P(('dp', 'fsdp')), may hold values from 0.099609375 to 1.8984375
- bias_table: bfloat16 [32, 12], replicated, may hold values from -6 to 6
Outputs:
- block_out: bfloat16 [64, 512, 768], P(('dp', 'fsdp'))
- loss: float32 [], replicated
- grad_tokens: float32 [64, 512, 768], P(('dp', 'fsdp'))
- grad_w_query: float32 [768, 768], P(('dp', 'fsdp'))
- grad_w_key: float32 [768, 768], P(('dp', 'fsdp'))
- grad_w_value: float32 [768, 768], P(('dp', 'fsdp'))
- grad_w_out: float32 [768, 768], P(('dp', 'fsdp'))
- grad_w_gate: float32 [768, 3072], P(('dp', 'fsdp'))
- grad_w_up: float32 [768, 3072], P(('dp', 'fsdp'))
- grad_w_down: float32 [3072, 768], P(('dp', 'fsdp'))
- grad_gain_attn: float32 [768], P(('dp', 'fsdp'))
- grad_gain_ff: float32 [768], P(('dp', 'fsdp'))
- grad_table: float32 [32, 12], replicated
The draws below stay inside these ranges and needn't reach their ends.
Inputs may be any that keep to these rules, and one draw needn't show every extreme that they name: Sequence s has lengths[s] valid tokens at its start; the other slots are padding.
All inputs are finite; a program needn't handle non-finite values.
Results may differ from the reference program's by a relative error of at most 0.013.
The reference program's roundings to bfloat16 on the way count: a program that leaves them out, or rounds other values in their place, can miss the bound.
Values may be sent and summed in bfloat16 or wider, within the bound.
No kernel may reach another device: no remote copies, remote signals or barrier semaphores. Data moves between devices by JAX's collectives and lax.ppermute only.
A program may use at most 256 MiB of HBM per device.

```python
import jax
import jax.numpy as jnp
from jax import lax

D = 768
H = 12
FF = 3072
BUCKETS = 32
MAXDIST = 128
LEN = 512
SEQS = 64
TOKENS = 32768


def draw_lengths(key, part):
    position = jnp.arange(SEQS, dtype=jnp.int32)
    base_length = LEN // 4 + 3 * LEN // 4 * position // max(SEQS - 1, 1)
    jitter = jax.random.randint(key, (SEQS,), 0, LEN // 8 + 1, dtype=jnp.int32)
    jitter = jnp.where(position == 0, 0, jitter)
    return jnp.minimum(base_length + jitter, LEN).astype(jnp.int32)


def shard_levels(rng, extent, pieces, smallest, top_value):
    loudness = 1.0
    for axis_at, parts in pieces:
        draws = jax.random.uniform(jax.random.fold_in(jax.random.fold_in(rng, 6), axis_at), (parts,), jnp.float32, smallest / len(pieces), top_value / len(pieces))
        loudness = loudness * jnp.repeat(jnp.exp(draws), extent[axis_at] // parts).reshape((-1,) + (1,) * (len(extent) - 1 - axis_at))
    return loudness


def bell_draw(key, dims, spread, limit, pieces=(), kind=jnp.bfloat16):
    entries = jax.random.normal(key, dims, jnp.float32) * spread
    if len(pieces) > 0:
        entries = shard_levels(key, dims, pieces, -0.22, 0.18) * entries
    return jnp.clip(entries, min=-limit, max=limit).astype(kind)


def setup_inputs(seed: int = 0) -> dict:
    keys = jax.random.split(jax.random.key(seed), 14)
    tokens = bell_draw(keys[0], (SEQS, LEN, D), 1.0, 6.0, ((0, 32),))
    teacher = bell_draw(keys[1], (SEQS, LEN, D), 1.0, 6.0, ((0, 32),))
    lengths = draw_lengths(jax.random.fold_in(keys[13], 71), 0)
    w_query = bell_draw(keys[3], (D, D), (0.5 * D ** -0.5), 0.109375, ((0, 32),))
    w_key = bell_draw(keys[4], (D, D), (0.5 * D ** -0.5), 0.109375, ((0, 32),))
    w_value = bell_draw(keys[5], (D, D), D ** -0.5, 0.21875, ((0, 32),))
    w_out = bell_draw(keys[6], (D, D), (D // 4) ** -0.5, 0.4375, ((0, 32),))
    w_gate = bell_draw(keys[7], (D, FF), D ** -0.5, 0.21875, ((0, 32),))
    w_up = bell_draw(keys[8], (D, FF), D ** -0.5, 0.21875, ((0, 32),))
    w_down = bell_draw(keys[9], (FF, D), (FF // 2) ** -0.5, 0.15625, ((0, 32),))
    gain_attn = jnp.clip(1.0 + 0.18 * jax.random.normal(keys[10], (D,), jnp.float32), 0.099609375, 1.8984375).astype(jnp.bfloat16)
    gain_ff = jnp.clip(1.0 + 0.18 * jax.random.normal(keys[11], (D,), jnp.float32), 0.099609375, 1.8984375).astype(jnp.bfloat16)
    bias_table = bell_draw(keys[12], (BUCKETS, H), 1.0, 6.0)
    return dict(tokens=tokens, teacher=teacher, lengths=lengths, w_query=w_query, w_key=w_key, w_value=w_value, w_out=w_out, w_gate=w_gate, w_up=w_up, w_down=w_down, gain_attn=gain_attn, gain_ff=gain_ff, bias_table=bias_table)


EPS = 1e-06
NEG = -1000000000.0

@jax.custom_vjp
def low(v):
    return lax.optimization_barrier(v.astype(jnp.bfloat16)).astype(jnp.float32)

@jax.custom_vjp
def low_back(v):
    return v

def low_keep(v):
    return (low(v), None)

def low_pass(kept, grad):
    return (grad,)

def back_keep(v):
    return (v, None)

def back_low(kept, grad):
    return (low(grad),)
low.defvjp(low_keep, low_pass)
low_back.defvjp(back_keep, back_low)

def cut_points():
    half_buckets = BUCKETS // 2
    exact_count = half_buckets // 2
    log_span = half_buckets - exact_count
    found = []
    for bucket_level in range(1, log_span):
        found.append(min((distance for distance in range(exact_count, MAXDIST + 1) if distance ** log_span * exact_count ** bucket_level >= MAXDIST ** bucket_level * exact_count ** log_span)))
    return found

def bucket_ids(start_row, row_count, key_count):
    half_buckets = BUCKETS // 2
    exact_count = half_buckets // 2
    offset = lax.broadcasted_iota(jnp.int32, (row_count, key_count), 1) - (start_row + lax.broadcasted_iota(jnp.int32, (row_count, key_count), 0))
    distance = jnp.abs(offset)
    far_level = jnp.full(distance.shape, exact_count, jnp.int32)
    for cut_point in cut_points():
        far_level = far_level + (distance >= cut_point).astype(jnp.int32)
    near_level = jnp.where(distance < exact_count, distance, jnp.minimum(far_level, half_buckets - 1))
    return (near_level + jnp.where(offset > 0, half_buckets, 0)).astype(jnp.int32)

def highest_dot(left, right):
    return jnp.dot(left, right, precision=lax.Precision.HIGHEST, preferred_element_type=jnp.float32)

def round_both(value):
    return low(low_back(value))

def normalize(stream, gain):
    scale = lax.rsqrt(lax.optimization_barrier(jnp.mean(stream * stream, axis=-1, keepdims=True)) + EPS)
    return low(gain * (stream * scale))

def one_sequence(params, x_seq, t_seq, length):
    w_query, w_key, w_value, w_out, w_gate, w_up, w_down, gain_attn, gain_ff, table = params
    seq_len = x_seq.shape[0]
    head_count = table.shape[1]
    head_dim = x_seq.shape[1] // head_count
    normed_attn = normalize(x_seq, gain_attn)
    query_heads = round_both(highest_dot(normed_attn, w_query)).reshape(seq_len, head_count, head_dim)
    key_heads = round_both(highest_dot(normed_attn, w_key)).reshape(seq_len, head_count, head_dim)
    value_heads = round_both(highest_dot(normed_attn, w_value)).reshape(seq_len, head_count, head_dim)
    bucket_of = bucket_ids(0, seq_len, seq_len)
    bias = jnp.transpose(table[bucket_of], (2, 0, 1))
    raw = jnp.einsum('ihd,jhd->hij', query_heads, key_heads, precision=lax.Precision.HIGHEST)
    scores = low_back(raw + bias)
    live_keys = lax.broadcasted_iota(jnp.int32, (1, 1, seq_len), 2) < length
    scores = jnp.where(live_keys, scores, NEG)
    probs = low(jax.nn.softmax(scores, axis=-1))
    attended = jnp.einsum('hij,jhd->ihd', probs, value_heads, precision=lax.Precision.HIGHEST)
    attended = round_both(attended.reshape(seq_len, head_count * head_dim))
    stream_mid = x_seq + low_back(highest_dot(attended, w_out))
    normed_ff = normalize(stream_mid, gain_ff)
    gate_pre = low_back(highest_dot(normed_ff, w_gate))
    up_pre = low_back(highest_dot(normed_ff, w_up))
    hidden = low(jax.nn.gelu(gate_pre, approximate=True) * up_pre)
    stream_out = stream_mid + low_back(highest_dot(hidden, w_down))
    live_rows = lax.broadcasted_iota(jnp.int32, (seq_len, 1), 0) < length
    error = jnp.sum(jnp.where(live_rows, (stream_out - t_seq) ** 2, 0.0))
    return (stream_out, error)

def reference(tokens, teacher, lengths, w_query, w_key, w_value, w_out, w_gate, w_up, w_down, gain_attn, gain_ff, bias_table):
    params = tuple((member.astype(jnp.float32) for member in (w_query, w_key, w_value, w_out, w_gate, w_up, w_down, gain_attn, gain_ff, bias_table)))
    stream_in = tokens.astype(jnp.float32)
    targets = teacher.astype(jnp.float32)
    valid_total = jnp.sum(lengths.astype(jnp.float32))
    step_fn = jax.checkpoint(one_sequence)

    def forward(x_all, *weights):

        def step(running, item):
            x_seq, t_seq, length = item
            stream_out, error = step_fn(weights, x_seq, t_seq, length)
            return (running + error, stream_out)
        total, outputs = lax.scan(step, jnp.zeros((), jnp.float32), (x_all, targets, lengths))
        return (outputs, total / valid_total)
    (outputs, loss), pullback = jax.vjp(forward, stream_in, *params)
    grads = pullback((jnp.zeros_like(outputs), jnp.asarray(TOKENS, jnp.float32)))
    return (outputs.astype(jnp.bfloat16), loss, grads[0], grads[1], grads[2], grads[3], grads[4], grads[5], grads[6], grads[7], grads[8], grads[9], grads[10])
```

```python
import jax
import jax.numpy as jnp
from jax import lax
from jax.experimental import pallas as pl
from jax.experimental.pallas import tpu as pltpu
from jax.sharding import PartitionSpec as P

BUCKETS = 32
MAXDIST = 128
EPS = 1e-06
NEG = -1000000000.0
TILE = 128
F32 = jnp.float32
BF16 = jnp.bfloat16


def cut_points():
    half_buckets = BUCKETS // 2
    exact_count = half_buckets // 2
    log_span = half_buckets - exact_count
    found = []
    for level in range(1, log_span):
        found.append(
            min(
                d
                for d in range(exact_count, MAXDIST + 1)
                if d**log_span * exact_count**level >= MAXDIST**level * exact_count**log_span
            )
        )
    return found


def bucket_of(offset):
    half_buckets = BUCKETS // 2
    exact_count = half_buckets // 2
    distance = jnp.abs(offset)
    far_level = jnp.full(distance.shape, exact_count, jnp.int32)
    for cut_point in cut_points():
        far_level = far_level + (distance >= cut_point).astype(jnp.int32)
    near = jnp.where(distance < exact_count, distance, jnp.minimum(far_level, half_buckets - 1))
    return near + jnp.where(offset > 0, half_buckets, 0)


def diagonal_onehot():
    shape = (5, TILE, TILE)
    offset = (
        (lax.broadcasted_iota(jnp.int32, shape, 0) - 2) * TILE
        + lax.broadcasted_iota(jnp.int32, shape, 1)
        - lax.broadcasted_iota(jnp.int32, shape, 2)
    )
    buckets = bucket_of(offset)
    return (buckets[None] == lax.broadcasted_iota(jnp.int32, (BUCKETS,) + shape, 0)).astype(BF16)


def swap_inner(value, axis):
    size = lax.axis_size(axis)
    return lax.ppermute(value, axis, [(i, i ^ 1) for i in range(size)])


def shift_outer(value, axis, step):
    size = lax.axis_size(axis)
    outer = size // 2
    return lax.ppermute(
        value, axis, [(i, ((i // 2 + step) % outer) * 2 + i % 2) for i in range(size)]
    )


def sum_everywhere(value):
    for axis in ("dp", "fsdp"):
        size = lax.axis_size(axis)
        bit = 1
        while bit < size:
            value = value + lax.ppermute(value, axis, [(i, i ^ bit) for i in range(size)])
            bit *= 2
    return value


def in_order(own, others, position):
    count = len(others) + 1
    pieces = [own] + list(others)
    placed = []
    for slot in range(count):
        chosen = pieces[0]
        for step in range(1, count):
            chosen = jnp.where((position - slot) % count == step, pieces[step], chosen)
        placed.append(chosen)
    return placed


def place_blocks(blocks, slots):
    count = len(blocks)
    shape = blocks[0].shape

    def body(slot_ref, *refs):
        sources, target, sems = refs[:count], refs[count], refs[count + 1]
        copies = [
            pltpu.make_async_copy(sources[k], target.at[slot_ref[k]], sems.at[k])
            for k in range(count)
        ]
        for copy in copies:
            copy.start()
        for copy in copies:
            copy.wait()

    return pl.pallas_call(
        body,
        out_shape=jax.ShapeDtypeStruct((count,) + shape, blocks[0].dtype),
        grid_spec=pltpu.PrefetchScalarGridSpec(
            num_scalar_prefetch=1,
            grid=(1,),
            in_specs=[pl.BlockSpec(memory_space=pl.ANY)] * count,
            out_specs=pl.BlockSpec(memory_space=pl.ANY),
            scratch_shapes=[pltpu.SemaphoreType.DMA((count,))],
        ),
        name="place_blocks",
    )(slots, *blocks)


def gather_rows(shard):
    dp_count, fsdp_count = lax.axis_size("dp"), lax.axis_size("fsdp")
    far_dp, far_fsdp = dp_count // 2, fsdp_count // 2
    dp_at, fsdp_at = lax.axis_index("dp"), lax.axis_index("fsdp")
    rows, columns = shard.shape
    along = in_order(
        shard, [shift_outer(shard, "fsdp", k) for k in range(1, far_fsdp)], fsdp_at // 2
    )
    line = jnp.stack(along)
    line_other = swap_inner(line, "fsdp")
    first = fsdp_at % 2 == 0
    plane = jnp.stack(
        [jnp.where(first, line, line_other), jnp.where(first, line_other, line)], axis=1
    ).reshape(fsdp_count * rows, columns)
    mine = [plane] + [shift_outer(plane, "dp", k) for k in range(1, far_dp)]
    theirs = [swap_inner(block, "dp") for block in mine]
    outer_at, inner_at = dp_at // 2, dp_at % 2
    outers = [(outer_at - k) % far_dp for k in range(far_dp)]
    slots = [o * 2 + inner_at for o in outers] + [o * 2 + 1 - inner_at for o in outers]
    whole = place_blocks(mine + theirs, jnp.stack(slots).astype(jnp.int32))
    return whole.reshape(dp_count * fsdp_count * rows, columns)


def pick(array, at):
    return lax.dynamic_index_in_dim(array, at, axis=0, keepdims=False)


def scatter_rows(members):
    dp_count, fsdp_count = lax.axis_size("dp"), lax.axis_size("fsdp")
    far_dp, far_fsdp = dp_count // 2, fsdp_count // 2
    dp_at, fsdp_at = lax.axis_index("dp"), lax.axis_index("fsdp")
    outer_at, inner_at = dp_at // 2, dp_at % 2
    depth_at, side_at = fsdp_at // 2, fsdp_at % 2
    row_block = members[0].shape[0] // dp_count
    share = row_block // fsdp_count

    def block(at_outer, at_inner):
        start = (at_outer * 2 + at_inner) * row_block
        parts = [lax.dynamic_slice_in_dim(m, start, row_block, axis=0) for m in members]
        return jnp.concatenate(parts, axis=1) if len(parts) > 1 else parts[0]

    outers = [(outer_at + k) % far_dp for k in range(far_dp)]
    from_pair = [swap_inner(block(o, 1 - inner_at), "dp") for o in outers]
    halves = [
        block(o, inner_at).astype(F32) + got.astype(F32) for o, got in zip(outers, from_pair)
    ]
    total = halves[0]
    for k in range(1, far_dp):
        total = total + shift_outer(halves[k].astype(BF16), "dp", k).astype(F32)
    columns = total.shape[1]
    total = total.reshape(far_fsdp, 2, share, columns)
    keep = jnp.where(side_at == 0, total[:, 0], total[:, 1])
    give = jnp.where(side_at == 0, total[:, 1], total[:, 0]).astype(BF16)
    keep = keep + swap_inner(give, "fsdp").astype(F32)
    result = pick(keep, depth_at)
    for k in range(1, far_fsdp):
        sent = pick(keep, (depth_at + k) % far_fsdp).astype(BF16)
        result = result + shift_outer(sent, "fsdp", k).astype(F32)
    return result


def dot_nt(left, right):
    return lax.dot_general(left, right, (((1,), (1,)), ((), ())), preferred_element_type=F32)


def dot_tn(left, right):
    return lax.dot_general(left, right, (((0,), (0,)), ((), ())), preferred_element_type=F32)


def dot_nn(left, right):
    return lax.dot_general(left, right, (((1,), (0,)), ((), ())), preferred_element_type=F32)


def block_kind(key_block, query_block):
    return max(-2, min(2, key_block - query_block)) + 2


def fill_bias(bias_ref, blocks_ref, head, count):
    for kb in range(count):
        for qb in range(count):
            bias_ref[head, kb * TILE : (kb + 1) * TILE, qb * TILE : (qb + 1) * TILE] = blocks_ref[
                head, block_kind(kb, qb)
            ]


def head_lanes(shape, head, head_dim):
    lane = lax.broadcasted_iota(jnp.int32, shape, 1)
    return (lane >= head * head_dim) & (lane < (head + 1) * head_dim)


def attention_forward(qkv, bias_blocks, lengths, head_count):
    seqs, seq_len, width3 = qkv.shape
    width = width3 // 3
    head_dim = width // head_count
    per_step = TILE // head_dim
    groups = head_count // per_step
    tiles = seq_len // TILE

    def body(len_ref, q_ref, k_ref, v_ref, blocks_ref, out_ref, lse_ref, bias_ref):
        seq = pl.program_id(1)

        @pl.when(seq == 0)
        def _():
            for head in range(per_step):
                fill_bias(bias_ref, blocks_ref, head, tiles)

        live = lax.broadcasted_iota(jnp.int32, (seq_len, seq_len), 0) < len_ref[seq]
        q, k = q_ref[0], k_ref[0]
        v_t = v_ref[0].T
        outs = []
        for head in range(per_step):
            q_head = jnp.where(head_lanes(q.shape, head, head_dim), q, jnp.zeros_like(q))
            scores = jnp.where(live, dot_nt(k, q_head) + bias_ref[head], NEG)
            top = jnp.max(scores, axis=0, keepdims=True)
            raised = jnp.exp(scores - top)
            total = jnp.sum(raised, axis=0, keepdims=True)
            probs = (raised * (1.0 / total)).astype(BF16)
            lse_ref[0, 0, head : head + 1, :] = top + jnp.log(total)
            outs.append(dot_nn(v_t[head * head_dim : (head + 1) * head_dim], probs))
        out_ref[0] = jnp.concatenate(outs, axis=0).T.astype(BF16)

    column = lambda part: pl.BlockSpec(
        (1, seq_len, TILE), lambda g, s, lens, part=part: (s, 0, part * groups + g)
    )
    return pl.pallas_call(
        body,
        out_shape=(
            jax.ShapeDtypeStruct((seqs, seq_len, width), BF16),
            jax.ShapeDtypeStruct((seqs, groups, per_step, seq_len), F32),
        ),
        grid_spec=pltpu.PrefetchScalarGridSpec(
            num_scalar_prefetch=1,
            grid=(groups, seqs),
            in_specs=[
                column(0),
                column(1),
                column(2),
                pl.BlockSpec((per_step, 5, TILE, TILE), lambda g, s, lens: (g, 0, 0, 0)),
            ],
            out_specs=(
                pl.BlockSpec((1, seq_len, TILE), lambda g, s, lens: (s, 0, g)),
                pl.BlockSpec((1, 1, per_step, seq_len), lambda g, s, lens: (s, g, 0, 0)),
            ),
            scratch_shapes=[pltpu.VMEM((per_step, seq_len, seq_len), F32)],
        ),
        compiler_params=pltpu.CompilerParams(dimension_semantics=("arbitrary", "arbitrary")),
        name="attention_forward",
    )(lengths, qkv, qkv, qkv, bias_blocks)


def attention_backward(qkv, grad_attended, lse, bias_blocks, lengths, head_count):
    seqs, seq_len, width3 = qkv.shape
    width = width3 // 3
    head_dim = width // head_count
    per_step = TILE // head_dim
    groups = head_count // per_step
    tiles = seq_len // TILE

    def body(
        len_ref, q_ref, k_ref, v_ref, do_ref, lse_ref, blocks_ref, grads_ref, diag_ref, bias_ref
    ):
        seq = pl.program_id(1)

        @pl.when(seq == 0)
        def _():
            for head in range(per_step):
                fill_bias(bias_ref, blocks_ref, head, tiles)
            diag_ref[...] = jnp.zeros_like(diag_ref)

        live = lax.broadcasted_iota(jnp.int32, (seq_len, seq_len), 0) < len_ref[seq]
        q, k, v, d_out = q_ref[0], k_ref[0], v_ref[0], do_ref[0]
        k_t = k.T
        d_key = jnp.zeros((seq_len, TILE), F32)
        d_value = jnp.zeros((seq_len, TILE), F32)
        d_query = []
        for head in range(per_step):
            lanes = head_lanes(q.shape, head, head_dim)
            q_head = jnp.where(lanes, q, jnp.zeros_like(q))
            do_head = jnp.where(lanes, d_out, jnp.zeros_like(d_out))
            scores = jnp.where(live, dot_nt(k, q_head) + bias_ref[head], NEG)
            probs = jnp.exp(scores - lse_ref[0, 0, head : head + 1, :])
            d_value = d_value + dot_nn(probs.astype(BF16), do_head)
            weighted = probs * dot_nt(v, do_head)
            d_scores = (weighted - probs * jnp.sum(weighted, axis=0, keepdims=True)).astype(BF16)
            d_key = d_key + dot_nn(d_scores, q_head)
            d_query.append(dot_nn(k_t[head * head_dim : (head + 1) * head_dim], d_scores))
            for kind in range(5):
                found = None
                for kb in range(tiles):
                    for qb in range(tiles):
                        if block_kind(kb, qb) == kind:
                            part = d_scores[
                                kb * TILE : (kb + 1) * TILE, qb * TILE : (qb + 1) * TILE
                            ].astype(F32)
                            found = part if found is None else found + part
                if found is not None:
                    diag_ref[head, kind] += found
        grads_ref[0, 0] = jnp.concatenate(d_query, axis=0).T.astype(BF16)
        grads_ref[1, 0] = d_key.astype(BF16)
        grads_ref[2, 0] = d_value.astype(BF16)

    column = lambda part: pl.BlockSpec(
        (1, seq_len, TILE), lambda g, s, lens, part=part: (s, 0, part * groups + g)
    )
    return pl.pallas_call(
        body,
        out_shape=(
            jax.ShapeDtypeStruct((3, seqs, seq_len, width), BF16),
            jax.ShapeDtypeStruct((head_count, 5, TILE, TILE), F32),
        ),
        grid_spec=pltpu.PrefetchScalarGridSpec(
            num_scalar_prefetch=1,
            grid=(groups, seqs),
            in_specs=[
                column(0),
                column(1),
                column(2),
                column(0),
                pl.BlockSpec((1, 1, per_step, seq_len), lambda g, s, lens: (s, g, 0, 0)),
                pl.BlockSpec((per_step, 5, TILE, TILE), lambda g, s, lens: (g, 0, 0, 0)),
            ],
            out_specs=(
                pl.BlockSpec((3, 1, seq_len, TILE), lambda g, s, lens: (0, s, 0, g)),
                pl.BlockSpec((per_step, 5, TILE, TILE), lambda g, s, lens: (g, 0, 0, 0)),
            ),
            scratch_shapes=[pltpu.VMEM((per_step, seq_len, seq_len), F32)],
        ),
        compiler_params=pltpu.CompilerParams(dimension_semantics=("arbitrary", "arbitrary")),
        name="attention_backward",
    )(lengths, qkv, qkv, qkv, grad_attended, lse, bias_blocks)


def norm_scale(stream):
    return lax.rsqrt(jnp.mean(stream * stream, axis=-1, keepdims=True) + EPS)


def gelu_parts(value):
    root = 0.7978845608028654
    inner = jnp.tanh(root * (value + 0.044715 * value * value * value))
    gelu = 0.5 * value * (1.0 + inner)
    slope = 0.5 * (1.0 + inner) + 0.5 * value * (1.0 - inner * inner) * root * (
        1.0 + 3.0 * 0.044715 * value * value
    )
    return gelu, slope


def on_device(
    tokens,
    teacher,
    lengths,
    w_query,
    w_key,
    w_value,
    w_out,
    w_gate,
    w_up,
    w_down,
    gain_attn,
    gain_ff,
    bias_table,
):
    seqs, seq_len, width = tokens.shape
    head_count = bias_table.shape[1]
    devices_all = lax.axis_size("dp") * lax.axis_size("fsdp")
    count = seqs * seq_len
    token_total = float(count * devices_all)

    gains = jnp.pad(jnp.stack([gain_attn, gain_ff], axis=1), ((0, 0), (0, TILE - 2)))
    first = gather_rows(jnp.concatenate([w_query, w_key, w_value, w_out, gains], axis=1))
    gate_full = gather_rows(w_gate)
    up_full = gather_rows(w_up)
    down_full = gather_rows(w_down)
    valid_total = sum_everywhere(jnp.sum(lengths.astype(F32)).reshape(1, 1))[0, 0]
    qkv_full = first[:, : 3 * width]
    out_full = first[:, 3 * width : 4 * width]
    gain_rows = first[:, 4 * width : 4 * width + 2].astype(F32)
    gain_a = gain_rows[:, 0].reshape(1, width)
    gain_f = gain_rows[:, 1].reshape(1, width)

    onehot = diagonal_onehot()
    bias_blocks = jnp.einsum("bh,bkij->hkij", bias_table, onehot, preferred_element_type=F32)

    stream_in = tokens.reshape(count, width).astype(F32)
    scale_attn = norm_scale(stream_in)
    unit_attn = stream_in * scale_attn
    normed_attn = (gain_a * unit_attn).astype(BF16)
    qkv = dot_nn(normed_attn, qkv_full).astype(BF16).reshape(seqs, seq_len, 3 * width)
    attended, lse = attention_forward(qkv, bias_blocks, lengths, head_count)
    attended = attended.reshape(count, width)
    stream_mid = stream_in + dot_nn(attended, out_full)
    scale_ff = norm_scale(stream_mid)
    unit_ff = stream_mid * scale_ff
    normed_ff = (gain_f * unit_ff).astype(BF16)
    gate_pre = dot_nn(normed_ff, gate_full)
    up_pre = dot_nn(normed_ff, up_full)
    gelu, slope = gelu_parts(gate_pre)
    hidden = (gelu * up_pre).astype(BF16)
    stream_out = stream_mid + dot_nn(hidden, down_full)

    live = (
        lax.broadcasted_iota(jnp.int32, (seqs, seq_len, 1), 1) < lengths[:, None, None]
    ).reshape(count, 1)
    missing = stream_out - teacher.reshape(count, width).astype(F32)
    error_sum = jnp.sum(jnp.where(live, missing * missing, 0.0))
    out_grad = jnp.where(live, (2.0 * token_total / valid_total) * missing, 0.0)
    low_out = out_grad.astype(BF16)

    grad_down = scatter_rows([dot_tn(hidden, low_out).astype(BF16)])
    grad_hidden = dot_nt(low_out, down_full)
    grad_gate_pre = (grad_hidden * up_pre * slope).astype(BF16)
    grad_up_pre = (grad_hidden * gelu).astype(BF16)
    grad_gate = scatter_rows([dot_tn(normed_ff, grad_gate_pre).astype(BF16)])
    grad_up = scatter_rows([dot_tn(normed_ff, grad_up_pre).astype(BF16)])
    grad_normed_ff = dot_nt(grad_gate_pre, gate_full) + dot_nt(grad_up_pre, up_full)
    grad_gain_ff = jnp.sum(grad_normed_ff * unit_ff, axis=0)
    scaled_ff = grad_normed_ff * gain_f
    grad_mid = out_grad + scale_ff * (
        scaled_ff - unit_ff * jnp.mean(scaled_ff * unit_ff, axis=-1, keepdims=True)
    )
    low_mid = grad_mid.astype(BF16)
    grad_out = scatter_rows([dot_tn(attended, low_mid).astype(BF16)])
    grad_attended = dot_nt(low_mid, out_full).astype(BF16).reshape(seqs, seq_len, width)
    grads_qkv, diagonals = attention_backward(
        qkv, grad_attended, lse, bias_blocks, lengths, head_count
    )
    table_grad = jnp.einsum(
        "bkij,hkij->bh", onehot.astype(F32), diagonals, precision=lax.Precision.HIGHEST
    )
    grads_qkv = grads_qkv.reshape(3, count, width)
    weight_grads = [dot_tn(normed_attn, grads_qkv[k]).astype(BF16) for k in range(3)]
    grad_normed_attn = (
        dot_nt(grads_qkv[0], qkv_full[:, :width])
        + dot_nt(grads_qkv[1], qkv_full[:, width : 2 * width])
        + dot_nt(grads_qkv[2], qkv_full[:, 2 * width :])
    )
    grad_gain_attn = jnp.sum(grad_normed_attn * unit_attn, axis=0)
    scaled_attn = grad_normed_attn * gain_a
    grad_input = grad_mid + scale_attn * (
        scaled_attn - unit_attn * jnp.mean(scaled_attn * unit_attn, axis=-1, keepdims=True)
    )
    gain_grads = jnp.pad(
        jnp.stack([grad_gain_attn, grad_gain_ff], axis=1), ((0, 0), (0, TILE - 2))
    ).astype(BF16)
    last = scatter_rows(weight_grads)
    last_gains = scatter_rows([gain_grads])

    sums = jnp.concatenate(
        [table_grad, jnp.broadcast_to(error_sum.reshape(1, 1), (1, head_count))], axis=0
    )
    sums = sum_everywhere(sums)
    loss = sums[BUCKETS, 0] / valid_total
    return (
        stream_out.astype(BF16).reshape(tokens.shape),
        loss,
        grad_input.reshape(tokens.shape),
        last[:, :width],
        last[:, width : 2 * width],
        last[:, 2 * width :],
        grad_out,
        grad_gate,
        grad_up,
        grad_down,
        last_gains[:, 0],
        last_gains[:, 1],
        sums[:BUCKETS],
    )


def solution(mesh):
    both = ("dp", "fsdp")
    rows = P(both, None)
    cube = P(both, None, None)
    return jax.shard_map(
        on_device,
        mesh=mesh,
        in_specs=(cube, cube, P(both)) + (rows,) * 7 + (P(both), P(both), P()),
        out_specs=(cube, P(), cube) + (rows,) * 7 + (P(both), P(both), P()),
        check_vma=False,
    )
```

```python
import jax
import jax.numpy as jnp
from jax import lax
from jax.experimental import pallas as pl
from jax.experimental.pallas import tpu as pltpu
from jax.sharding import PartitionSpec as P

BUCKETS = 32
MAXDIST = 128
EPS = 1e-06
NEG = -1000000000.0
TILE = 128
F32 = jnp.float32
BF16 = jnp.bfloat16


def cut_points():
    half_buckets = BUCKETS // 2
    exact_count = half_buckets // 2
    log_span = half_buckets - exact_count
    found = []
    for level in range(1, log_span):
        found.append(
            min(
                d
                for d in range(exact_count, MAXDIST + 1)
                if d**log_span * exact_count**level >= MAXDIST**level * exact_count**log_span
            )
        )
    return found


def bucket_of(offset):
    half_buckets = BUCKETS // 2
    exact_count = half_buckets // 2
    distance = jnp.abs(offset)
    far_level = jnp.full(distance.shape, exact_count, jnp.int32)
    for cut_point in cut_points():
        far_level = far_level + (distance >= cut_point).astype(jnp.int32)
    near = jnp.where(distance < exact_count, distance, jnp.minimum(far_level, half_buckets - 1))
    return near + jnp.where(offset > 0, half_buckets, 0)


def diagonal_onehot():
    shape = (5, TILE, TILE)
    offset = (
        (lax.broadcasted_iota(jnp.int32, shape, 0) - 2) * TILE
        + lax.broadcasted_iota(jnp.int32, shape, 1)
        - lax.broadcasted_iota(jnp.int32, shape, 2)
    )
    buckets = bucket_of(offset)
    return (buckets[None] == lax.broadcasted_iota(jnp.int32, (BUCKETS,) + shape, 0)).astype(BF16)


def swap_inner(value, axis):
    size = lax.axis_size(axis)
    return lax.ppermute(value, axis, [(i, i ^ 1) for i in range(size)])


def shift_outer(value, axis, step):
    size = lax.axis_size(axis)
    outer = size // 2
    return lax.ppermute(
        value, axis, [(i, ((i // 2 + step) % outer) * 2 + i % 2) for i in range(size)]
    )


def sum_everywhere(value):
    for axis in ("dp", "fsdp"):
        size = lax.axis_size(axis)
        bit = 1
        while bit < size:
            value = value + lax.ppermute(value, axis, [(i, i ^ bit) for i in range(size)])
            bit *= 2
    return value


def in_order(own, others, position):
    count = len(others) + 1
    pieces = [own] + list(others)
    placed = []
    for slot in range(count):
        chosen = pieces[0]
        for step in range(1, count):
            chosen = jnp.where((position - slot) % count == step, pieces[step], chosen)
        placed.append(chosen)
    return placed


def place_blocks(blocks, slots):
    count = len(blocks)
    rows, columns = blocks[0].shape
    chunk = columns
    for parts in (4, 5, 3, 2):
        if columns % (parts * TILE) == 0:
            chunk = columns // parts
            break

    def body(slot_ref, *refs):
        for k in range(count):

            @pl.when(pl.program_id(1) == k)
            def _():
                refs[count][0] = refs[k][...]

    return pl.pallas_call(
        body,
        out_shape=jax.ShapeDtypeStruct((count, rows, columns), blocks[0].dtype),
        grid_spec=pltpu.PrefetchScalarGridSpec(
            num_scalar_prefetch=1,
            grid=(columns // chunk, count),
            in_specs=[pl.BlockSpec((rows, chunk), lambda j, i, slot_ref: (0, j))] * count,
            out_specs=pl.BlockSpec((1, rows, chunk), lambda j, i, slot_ref: (slot_ref[i], 0, j)),
        ),
        name="place_blocks",
    )(slots, *blocks)


def tied(*values):
    return lax.optimization_barrier(values)


class Gather:
    def __init__(self, shard):
        self.shard = shard
        self.dp_at, self.fsdp_at = lax.axis_index("dp"), lax.axis_index("fsdp")
        self.far_dp = lax.axis_size("dp") // 2
        self.far_fsdp = lax.axis_size("fsdp") // 2

    def depth(self):
        others = [shift_outer(self.shard, "fsdp", k) for k in range(1, self.far_fsdp)]
        self.lines = [jnp.stack(in_order(self.shard, others, self.fsdp_at // 2))]

    def across(self):
        self.lines = self.lines + [
            shift_outer(self.lines[0], "dp", k) for k in range(1, self.far_dp)
        ]

    def side(self):
        first = self.fsdp_at % 2 == 0
        planes = []
        for line in self.lines:
            other = swap_inner(line, "fsdp")
            plane = jnp.stack(
                [jnp.where(first, line, other), jnp.where(first, other, line)], axis=1
            )
            planes.append(plane.reshape(-1, line.shape[-1]))
        self.lines = planes

    def pair(self):
        inner_at = self.dp_at % 2
        theirs = [swap_inner(block, "dp") for block in self.lines]
        outers = [(self.dp_at // 2 - k) % self.far_dp for k in range(self.far_dp)]
        slots = [o * 2 + inner_at for o in outers] + [o * 2 + 1 - inner_at for o in outers]
        whole = place_blocks(self.lines + theirs, jnp.stack(slots).astype(jnp.int32))
        return whole.reshape(-1, self.shard.shape[-1])


def pick(array, at):
    return lax.dynamic_index_in_dim(array, at, axis=0, keepdims=False)


def tied_with(works, *values):
    held = [list(work.held) for work in works]
    held, values = lax.optimization_barrier((held, values))
    for work, got in zip(works, held):
        work.held = got
    return values


class Scatter:
    def __init__(self, members):
        self.members = members
        dp_count, fsdp_count = lax.axis_size("dp"), lax.axis_size("fsdp")
        self.far_dp, self.far_fsdp = dp_count // 2, fsdp_count // 2
        dp_at, fsdp_at = lax.axis_index("dp"), lax.axis_index("fsdp")
        self.outer_at, self.inner_at = dp_at // 2, dp_at % 2
        self.depth_at, self.side_at = fsdp_at // 2, fsdp_at % 2
        self.row_block = members[0].shape[0] // dp_count
        self.share = self.row_block // fsdp_count
        self.outers = [(self.outer_at + k) % self.far_dp for k in range(self.far_dp)]
        self.held = []

    def block(self, at_outer, at_inner):
        start = (at_outer * 2 + at_inner) * self.row_block
        parts = [
            lax.dynamic_slice_in_dim(m, start, self.row_block, axis=0) for m in self.members
        ]
        return jnp.concatenate(parts, axis=1) if len(parts) > 1 else parts[0]

    def pair(self):
        self.held = [swap_inner(self.block(o, 1 - self.inner_at), "dp") for o in self.outers]

    def paired(self):
        return [
            self.block(o, self.inner_at).astype(F32) + got.astype(F32)
            for o, got in zip(self.outers, self.held)
        ]

    def across(self, parts):
        self.kept = parts[0]
        self.held = [
            shift_outer(parts[k].astype(BF16), "dp", k) for k in range(1, self.far_dp)
        ]

    def summed(self):
        total = self.kept
        for got in self.held:
            total = total + got.astype(F32)
        return total

    def side(self, parts):
        parts = [part.reshape(self.far_fsdp, 2, self.share, -1) for part in parts]
        self.kept_sides = [
            jnp.where(self.side_at == 0, part[:, 0], part[:, 1]) for part in parts
        ]
        self.held = [
            swap_inner(
                jnp.where(self.side_at == 0, part[:, 1], part[:, 0]).astype(BF16), "fsdp"
            )
            for part in parts
        ]

    def sided(self):
        return [kept + got.astype(F32) for kept, got in zip(self.kept_sides, self.held)]

    def depth(self, total):
        self.kept = pick(total, self.depth_at)
        self.held = [
            shift_outer(
                pick(total, (self.depth_at + k) % self.far_fsdp).astype(BF16), "fsdp", k
            )
            for k in range(1, self.far_fsdp)
        ]


def dot_nt(left, right):
    return lax.dot_general(left, right, (((1,), (1,)), ((), ())), preferred_element_type=F32)


def dot_tn(left, right):
    return lax.dot_general(left, right, (((0,), (0,)), ((), ())), preferred_element_type=F32)


def dot_nn(left, right):
    return lax.dot_general(left, right, (((1,), (0,)), ((), ())), preferred_element_type=F32)


def block_kind(key_block, query_block):
    return max(-2, min(2, key_block - query_block)) + 2


def fill_bias(bias_ref, blocks_ref, head, count):
    for kb in range(count):
        for qb in range(count):
            bias_ref[head, kb * TILE : (kb + 1) * TILE, qb * TILE : (qb + 1) * TILE] = blocks_ref[
                head, block_kind(kb, qb)
            ]


def head_lanes(shape, head, head_dim):
    lane = lax.broadcasted_iota(jnp.int32, shape, 1)
    return (lane >= head * head_dim) & (lane < (head + 1) * head_dim)


def attention_forward(qkv, bias_blocks, lengths, head_count):
    seqs, seq_len, width3 = qkv.shape
    width = width3 // 3
    head_dim = width // head_count
    per_step = TILE // head_dim
    groups = head_count // per_step
    tiles = seq_len // TILE

    def body(len_ref, q_ref, k_ref, v_ref, blocks_ref, out_ref, lse_ref, bias_ref):
        seq = pl.program_id(1)

        @pl.when(seq == 0)
        def _():
            for head in range(per_step):
                fill_bias(bias_ref, blocks_ref, head, tiles)

        live = lax.broadcasted_iota(jnp.int32, (seq_len, seq_len), 0) < len_ref[seq]
        q, k = q_ref[0], k_ref[0]
        v_t = v_ref[0].T
        outs = []
        for head in range(per_step):
            q_head = jnp.where(head_lanes(q.shape, head, head_dim), q, jnp.zeros_like(q))
            scores = jnp.where(live, dot_nt(k, q_head) + bias_ref[head], NEG)
            top = jnp.max(scores, axis=0, keepdims=True)
            raised = jnp.exp(scores - top)
            total = jnp.sum(raised, axis=0, keepdims=True)
            probs = (raised * (1.0 / total)).astype(BF16)
            lse_ref[0, 0, head : head + 1, :] = top + jnp.log(total)
            outs.append(dot_nn(v_t[head * head_dim : (head + 1) * head_dim], probs))
        out_ref[0] = jnp.concatenate(outs, axis=0).T.astype(BF16)

    column = lambda part: pl.BlockSpec(
        (1, seq_len, TILE), lambda g, s, lens, part=part: (s, 0, part * groups + g)
    )
    return pl.pallas_call(
        body,
        out_shape=(
            jax.ShapeDtypeStruct((seqs, seq_len, width), BF16),
            jax.ShapeDtypeStruct((seqs, groups, per_step, seq_len), F32),
        ),
        grid_spec=pltpu.PrefetchScalarGridSpec(
            num_scalar_prefetch=1,
            grid=(groups, seqs),
            in_specs=[
                column(0),
                column(1),
                column(2),
                pl.BlockSpec((per_step, 5, TILE, TILE), lambda g, s, lens: (g, 0, 0, 0)),
            ],
            out_specs=(
                pl.BlockSpec((1, seq_len, TILE), lambda g, s, lens: (s, 0, g)),
                pl.BlockSpec((1, 1, per_step, seq_len), lambda g, s, lens: (s, g, 0, 0)),
            ),
            scratch_shapes=[pltpu.VMEM((per_step, seq_len, seq_len), F32)],
        ),
        compiler_params=pltpu.CompilerParams(dimension_semantics=("arbitrary", "arbitrary")),
        name="attention_forward",
    )(lengths, qkv, qkv, qkv, bias_blocks)


def attention_backward(qkv, grad_attended, lse, bias_blocks, lengths, head_count):
    seqs, seq_len, width3 = qkv.shape
    width = width3 // 3
    head_dim = width // head_count
    per_step = TILE // head_dim
    groups = head_count // per_step
    tiles = seq_len // TILE

    def body(
        len_ref, q_ref, k_ref, v_ref, do_ref, lse_ref, blocks_ref, grads_ref, diag_ref, bias_ref
    ):
        seq = pl.program_id(1)

        @pl.when(seq == 0)
        def _():
            for head in range(per_step):
                fill_bias(bias_ref, blocks_ref, head, tiles)
            diag_ref[...] = jnp.zeros_like(diag_ref)

        live = lax.broadcasted_iota(jnp.int32, (seq_len, seq_len), 0) < len_ref[seq]
        q, k, v, d_out = q_ref[0], k_ref[0], v_ref[0], do_ref[0]
        k_t = k.T
        d_key = jnp.zeros((seq_len, TILE), F32)
        d_value = jnp.zeros((seq_len, TILE), F32)
        d_query = []
        for head in range(per_step):
            lanes = head_lanes(q.shape, head, head_dim)
            q_head = jnp.where(lanes, q, jnp.zeros_like(q))
            do_head = jnp.where(lanes, d_out, jnp.zeros_like(d_out))
            scores = jnp.where(live, dot_nt(k, q_head) + bias_ref[head], NEG)
            probs = jnp.exp(scores - lse_ref[0, 0, head : head + 1, :])
            d_value = d_value + dot_nn(probs.astype(BF16), do_head)
            weighted = probs * dot_nt(v, do_head)
            d_scores = (weighted - probs * jnp.sum(weighted, axis=0, keepdims=True)).astype(BF16)
            d_key = d_key + dot_nn(d_scores, q_head)
            d_query.append(dot_nn(k_t[head * head_dim : (head + 1) * head_dim], d_scores))
            for kind in range(5):
                found = None
                for kb in range(tiles):
                    for qb in range(tiles):
                        if block_kind(kb, qb) == kind:
                            part = d_scores[
                                kb * TILE : (kb + 1) * TILE, qb * TILE : (qb + 1) * TILE
                            ].astype(F32)
                            found = part if found is None else found + part
                if found is not None:
                    diag_ref[head, kind] += found
        grads_ref[0, 0] = jnp.concatenate(d_query, axis=0).T.astype(BF16)
        grads_ref[1, 0] = d_key.astype(BF16)
        grads_ref[2, 0] = d_value.astype(BF16)

    column = lambda part: pl.BlockSpec(
        (1, seq_len, TILE), lambda g, s, lens, part=part: (s, 0, part * groups + g)
    )
    return pl.pallas_call(
        body,
        out_shape=(
            jax.ShapeDtypeStruct((3, seqs, seq_len, width), BF16),
            jax.ShapeDtypeStruct((head_count, 5, TILE, TILE), F32),
        ),
        grid_spec=pltpu.PrefetchScalarGridSpec(
            num_scalar_prefetch=1,
            grid=(groups, seqs),
            in_specs=[
                column(0),
                column(1),
                column(2),
                column(0),
                pl.BlockSpec((1, 1, per_step, seq_len), lambda g, s, lens: (s, g, 0, 0)),
                pl.BlockSpec((per_step, 5, TILE, TILE), lambda g, s, lens: (g, 0, 0, 0)),
            ],
            out_specs=(
                pl.BlockSpec((3, 1, seq_len, TILE), lambda g, s, lens: (0, s, 0, g)),
                pl.BlockSpec((per_step, 5, TILE, TILE), lambda g, s, lens: (g, 0, 0, 0)),
            ),
            scratch_shapes=[pltpu.VMEM((per_step, seq_len, seq_len), F32)],
        ),
        compiler_params=pltpu.CompilerParams(dimension_semantics=("arbitrary", "arbitrary")),
        name="attention_backward",
    )(lengths, qkv, qkv, qkv, grad_attended, lse, bias_blocks)


def norm_scale(stream):
    return lax.rsqrt(jnp.mean(stream * stream, axis=-1, keepdims=True) + EPS)


def gelu_parts(value):
    root = 0.7978845608028654
    inner = jnp.tanh(root * (value + 0.044715 * value * value * value))
    gelu = 0.5 * value * (1.0 + inner)
    slope = 0.5 * (1.0 + inner) + 0.5 * value * (1.0 - inner * inner) * root * (
        1.0 + 3.0 * 0.044715 * value * value
    )
    return gelu, slope


def on_device(
    tokens,
    teacher,
    lengths,
    w_query,
    w_key,
    w_value,
    w_out,
    w_gate,
    w_up,
    w_down,
    gain_attn,
    gain_ff,
    bias_table,
):
    seqs, seq_len, width = tokens.shape
    head_count = bias_table.shape[1]
    devices_all = lax.axis_size("dp") * lax.axis_size("fsdp")
    count = seqs * seq_len
    token_total = float(count * devices_all)

    gains = jnp.pad(jnp.stack([gain_attn, gain_ff], axis=1), ((0, 0), (0, TILE - 2)))
    early = Gather(jnp.concatenate([w_query, w_key, w_value, w_out, gains], axis=1))
    gate = Gather(w_gate)
    up = Gather(w_up)
    down = Gather(w_down)
    early.depth()
    early.lines[0], gate.shard, up.shard = tied(early.lines[0], gate.shard, up.shard)
    early.side()
    gate.depth()
    early.lines[0], gate.lines[0] = tied(early.lines[0], gate.lines[0])
    early.across()
    up.depth()
    gate.side()
    early.lines[1], up.lines[0], gate.lines[0], down.shard = tied(
        early.lines[1], up.lines[0], gate.lines[0], down.shard
    )
    first = early.pair()
    first, up.lines[0], gate.lines[0], down.shard = tied(
        first, up.lines[0], gate.lines[0], down.shard
    )
    gate.across()
    up.across()
    down.depth()
    valid_total = sum_everywhere(jnp.sum(lengths.astype(F32)).reshape(1, 1))[0, 0]
    qkv_full = first[:, : 3 * width]
    out_full = first[:, 3 * width : 4 * width]
    gain_rows = first[:, 4 * width : 4 * width + 2].astype(F32)
    gain_a = gain_rows[:, 0].reshape(1, width)
    gain_f = gain_rows[:, 1].reshape(1, width)

    onehot = diagonal_onehot()
    bias_blocks = jnp.einsum("bh,bkij->hkij", bias_table, onehot, preferred_element_type=F32)

    stream_in = tokens.reshape(count, width).astype(F32)
    scale_attn = norm_scale(stream_in)
    unit_attn = stream_in * scale_attn
    normed_attn = (gain_a * unit_attn).astype(BF16)
    qkv = dot_nn(normed_attn, qkv_full).astype(BF16).reshape(seqs, seq_len, 3 * width)
    attended, lse = attention_forward(qkv, bias_blocks, lengths, head_count)
    attended, gate.lines[1], up.lines[1], down.lines[0] = tied(
        attended, gate.lines[1], up.lines[1], down.lines[0]
    )
    up.side()
    down.side()
    gate_full = gate.pair()
    attended = attended.reshape(count, width)
    stream_mid = stream_in + dot_nn(attended, out_full)
    scale_ff = norm_scale(stream_mid)
    unit_ff = stream_mid * scale_ff
    normed_ff = (gain_f * unit_ff).astype(BF16)
    gate_full, up.lines[0], up.lines[1], down.lines[0] = tied(
        gate_full, up.lines[0], up.lines[1], down.lines[0]
    )
    down.across()
    up_full = up.pair()
    gate_pre = dot_nn(normed_ff, gate_full)
    up_pre = dot_nn(normed_ff, up_full)
    up_full, down.lines[1] = tied(up_full, down.lines[1])
    down_full = down.pair()
    gelu, slope = gelu_parts(gate_pre)
    hidden = (gelu * up_pre).astype(BF16)
    stream_out = stream_mid + dot_nn(hidden, down_full)

    live = (
        lax.broadcasted_iota(jnp.int32, (seqs, seq_len, 1), 1) < lengths[:, None, None]
    ).reshape(count, 1)
    missing = stream_out - teacher.reshape(count, width).astype(F32)
    error_sum = jnp.sum(jnp.where(live, missing * missing, 0.0))
    out_grad = jnp.where(live, (2.0 * token_total / valid_total) * missing, 0.0)
    low_out = out_grad.astype(BF16)

    down_terms = dot_tn(hidden, low_out).astype(BF16)
    low_out, down_terms = tied(low_out, down_terms)
    down_sum = Scatter([down_terms])
    down_sum.pair()
    grad_hidden = dot_nt(low_out, down_full)
    grad_gate_pre = (grad_hidden * up_pre * slope).astype(BF16)
    grad_up_pre = (grad_hidden * gelu).astype(BF16)
    gate_terms = dot_tn(normed_ff, grad_gate_pre).astype(BF16)
    grad_gate_pre, grad_up_pre, gate_terms = tied_with(
        [down_sum], grad_gate_pre, grad_up_pre, gate_terms
    )
    down_sum.across(down_sum.paired())
    gate_sum = Scatter([gate_terms])
    gate_sum.pair()
    up_terms = dot_tn(normed_ff, grad_up_pre).astype(BF16)
    grad_normed_ff = dot_nt(grad_gate_pre, gate_full)
    up_terms, grad_normed_ff, grad_up_pre = tied_with(
        [down_sum, gate_sum], up_terms, grad_normed_ff, grad_up_pre
    )
    down_sum.side([down_sum.summed()])
    gate_sum.across(gate_sum.paired())
    up_sum = Scatter([up_terms])
    up_sum.pair()
    grad_normed_ff = grad_normed_ff + dot_nt(grad_up_pre, up_full)
    grad_gain_ff = jnp.sum(grad_normed_ff * unit_ff, axis=0)
    scaled_ff = grad_normed_ff * gain_f
    grad_mid = out_grad + scale_ff * (
        scaled_ff - unit_ff * jnp.mean(scaled_ff * unit_ff, axis=-1, keepdims=True)
    )
    low_mid = grad_mid.astype(BF16)
    grad_attended = dot_nt(low_mid, out_full).astype(BF16).reshape(seqs, seq_len, width)
    grad_attended, low_mid, grad_gain_ff = tied_with(
        [down_sum, up_sum], grad_attended, low_mid, grad_gain_ff
    )
    down_sum.depth(down_sum.sided()[0])
    up_sum.side(up_sum.paired())
    grads_qkv, diagonals = attention_backward(
        qkv, grad_attended, lse, bias_blocks, lengths, head_count
    )
    grads_qkv, diagonals = tied_with([down_sum, up_sum, gate_sum], grads_qkv, diagonals)
    grad_down = down_sum.summed()
    gate_sum.side([gate_sum.summed()])
    up_sum.across(up_sum.sided())
    grads_qkv = grads_qkv.reshape(3, count, width)
    last_terms = [dot_tn(normed_attn, grads_qkv[k]).astype(BF16) for k in range(3)]
    last_terms.append(dot_tn(attended, low_mid).astype(BF16))
    *last_terms, grads_qkv = tied_with([gate_sum, up_sum], *last_terms, grads_qkv)
    last_sum = Scatter(last_terms)
    last_sum.pair()
    gate_sum.depth(gate_sum.sided()[0])
    up_sum.depth(up_sum.summed())
    grad_normed_attn = (
        dot_nt(grads_qkv[0], qkv_full[:, :width])
        + dot_nt(grads_qkv[1], qkv_full[:, width : 2 * width])
        + dot_nt(grads_qkv[2], qkv_full[:, 2 * width :])
    )
    (grad_normed_attn,) = tied_with([last_sum], grad_normed_attn)
    last_sum.across(last_sum.paired())
    grad_gain_attn = jnp.sum(grad_normed_attn * unit_attn, axis=0)
    scaled_attn = grad_normed_attn * gain_a
    grad_input = grad_mid + scale_attn * (
        scaled_attn - unit_attn * jnp.mean(scaled_attn * unit_attn, axis=-1, keepdims=True)
    )
    table_grad = jnp.einsum(
        "bkij,hkij->bh", onehot.astype(F32), diagonals, precision=lax.Precision.HIGHEST
    )
    grad_gate = gate_sum.summed()
    grad_up = up_sum.summed()
    last_sum.side([last_sum.summed()])
    last_sum.depth(last_sum.sided()[0])
    last = last_sum.summed()
    sums = sum_everywhere(
        jnp.concatenate(
            [
                jnp.pad(table_grad, ((0, 0), (0, width - head_count))),
                grad_gain_attn[None],
                grad_gain_ff[None],
                jnp.broadcast_to(error_sum.reshape(1, 1), (1, width)),
            ],
            axis=0,
        )
    )
    loss = sums[BUCKETS + 2, 0] / valid_total
    share = gain_attn.shape[0]
    start = (lax.axis_index("dp") * lax.axis_size("fsdp") + lax.axis_index("fsdp")) * share
    own_gains = lax.dynamic_slice_in_dim(sums[BUCKETS : BUCKETS + 2], start, share, axis=1)
    return (
        stream_out.astype(BF16).reshape(tokens.shape),
        loss,
        grad_input.reshape(tokens.shape),
        last[:, :width],
        last[:, width : 2 * width],
        last[:, 2 * width : 3 * width],
        last[:, 3 * width :],
        grad_gate,
        grad_up,
        grad_down,
        own_gains[0],
        own_gains[1],
        sums[:BUCKETS, :head_count],
    )


def solution(mesh):
    both = ("dp", "fsdp")
    rows = P(both, None)
    cube = P(both, None, None)
    return jax.shard_map(
        on_device,
        mesh=mesh,
        in_specs=(cube, cube, P(both)) + (rows,) * 7 + (P(both), P(both), P()),
        out_specs=(cube, P(), cube) + (rows,) * 7 + (P(both), P(both), P()),
        check_vma=False,
    )
```
